32 devices in a mesh: dp: 8 (over z, x), tensor: 4 (over y, core).
Axes of the slice: x: 2, y: 2, z: 4, core: 2. Of those that a mesh axis runs over, the one named last changes fastest.
Arguments:
- queries: bfloat16 [256, 32, 2048], P('dp', None, 'tensor'), may hold values from -8 to 8
- keys: bfloat16 [256, 32, 512], P('dp', None, 'tensor'), may hold values from -8 to 8
- values: bfloat16 [256, 32, 512], P('dp', None, 'tensor'), may hold values from -6 to 6
- out_weight: bfloat16 [2048, 4096], P(None, 'tensor'), may hold values from -0.125 to 0.125
- dest_slot: int32 [256], P('dp'), may hold values from 0 to 31, as said below
- pack_slot: int32 [8, 32], P('dp'), may hold values from 0 to 31, as said below
- seq_start: int32 [8, 32], P('dp'), may hold values from 0 to 1024, as said below
- seq_len: int32 [8, 32], P('dp'), may hold values from 0 to 1024, as said below
Outputs:
- projected: bfloat16 [256, 32, 4096], P('dp', None, 'tensor')
The draws below stay inside these ranges and needn't reach their ends.
Inputs may be any that keep to these rules, and one draw needn't show every extreme that they name: Block i of loader l goes to pack dest_slot[l * 32 + i] // 4; the 32 values of one loader are distinct. pack_slot[p, s] = l * 4 + m names the block of loader l whose dest_slot is p * 4 + m; the values of one pack are distinct, and every block of every loader fills exactly one position of one pack, so each pack holds exactly 32 blocks. Multiples of 32; seq_start[p, 0] = 0, the used entries rise, and a sequence's blocks run up to the next used start (or to the pack's end); the entries after the used ones equal 1024. Some pack holds a single sequence of all its blocks. `seq_len`: for a used sequence of b blocks, from b * 32 - 32 // 4 + 1 to b * 32; 0 for unused entries.
All inputs are finite; a program needn't handle non-finite values.
Results may differ from the reference program's by a relative error of at most 0.01.
Values may be sent and summed in bfloat16 or wider, within the bound.
No kernel may reach another device: no remote copies, remote signals or barrier semaphores. Data moves between devices by JAX's collectives and lax.ppermute only.
A program may use at most 64 MiB of HBM per device.

```python
import jax
import jax.numpy as jnp
from jax import lax

D = 4096
HEAD_SIZE = 128
QUERY_HEADS = 16
KEY_VALUE_HEADS = 4
BLOCK_ROWS = 32
LOADER_BLOCKS = 32
CAP = 4
TOTAL_BLOCKS = 256
N_DP = 8


def local_order(sub_key):
    return jax.random.permutation(sub_key, LOADER_BLOCKS)


def routing_tables(key):
    base_key = jax.random.fold_in(key, 7001)
    keys_four = jax.random.split(base_key, 4)
    order_a = jax.random.permutation(keys_four[0], N_DP).astype(jnp.int32)
    order_b = jax.random.permutation(keys_four[1], N_DP).astype(jnp.int32)
    offsets = jax.random.permutation(keys_four[2], N_DP).astype(jnp.int32)
    position = jnp.arange(LOADER_BLOCKS, dtype=jnp.int32)
    shift_of = offsets[position % N_DP]
    layer_of = position // N_DP
    loader_of = order_a[(order_b[:, None] + shift_of[None, :]) % N_DP]
    pack_table = (loader_of * CAP + layer_of[None, :]).astype(jnp.int32)
    inverse_a = jnp.argsort(order_a).astype(jnp.int32)
    inverse_b = jnp.argsort(order_b).astype(jnp.int32)
    pack_of = inverse_b[(inverse_a[:, None] - shift_of[None, :]) % N_DP]
    sending = (pack_of * CAP + layer_of[None, :]).astype(jnp.int32)
    local_orders = jax.vmap(local_order)(jax.random.split(keys_four[3], N_DP)).astype(jnp.int32)
    loader_rows = jnp.arange(N_DP, dtype=jnp.int32)[:, None] * jnp.ones((1, LOADER_BLOCKS), jnp.int32)
    dest_table = jnp.zeros((N_DP, LOADER_BLOCKS), jnp.int32).at[loader_rows, local_orders].set(sending)
    return (dest_table.reshape(TOTAL_BLOCKS), pack_table)


def segment_tables(key):
    base_key = jax.random.fold_in(key, 7002)
    keys_four = jax.random.split(base_key, 4)
    cut_rates = jax.random.randint(keys_four[0], (N_DP,), 0, 9)
    single_pack = jax.random.randint(keys_four[1], (), 0, N_DP)
    cut_rates = jnp.where(jnp.arange(N_DP) == single_pack, 0, cut_rates)
    coin_draws = jax.random.randint(keys_four[2], (N_DP, LOADER_BLOCKS), 0, 8)
    position = jnp.arange(LOADER_BLOCKS, dtype=jnp.int32)
    boundary = (coin_draws < cut_rates[:, None]) | (position[None, :] == 0)
    starts_block = jnp.sort(jnp.where(boundary, position[None, :], LOADER_BLOCKS), axis=1).astype(jnp.int32)
    following = jnp.concatenate([starts_block[:, 1:], jnp.full((N_DP, 1), LOADER_BLOCKS, jnp.int32)], axis=1)
    counts = jnp.where(starts_block < LOADER_BLOCKS, following - starts_block, 0)
    padding = jax.random.randint(keys_four[3], (N_DP, LOADER_BLOCKS), 0, max(BLOCK_ROWS // 4, 1))
    lengths = jnp.where(counts > 0, counts * BLOCK_ROWS - padding, 0).astype(jnp.int32)
    return ((starts_block * BLOCK_ROWS).astype(jnp.int32), lengths)


def draw_dest_slot(key, part):
    return routing_tables(key)[0]


def draw_pack_slot(key, part):
    return routing_tables(key)[1]


def draw_seq_start(key, part):
    return segment_tables(key)[0]


def draw_seq_len(key, part):
    return segment_tables(key)[1]


def draw_queries(key, part):
    noise_key = jax.random.fold_in(key, 7004)
    overall_shape = (TOTAL_BLOCKS, BLOCK_ROWS, QUERY_HEADS * HEAD_SIZE)
    base_draw = jnp.clip(jax.random.normal(noise_key, overall_shape, jnp.float32), -6.0, 6.0)
    return base_draw.astype(jnp.bfloat16)


def draw_keys(key, part):
    noise_key = jax.random.fold_in(key, 7006)
    overall_shape = (TOTAL_BLOCKS, BLOCK_ROWS, KEY_VALUE_HEADS * HEAD_SIZE)
    base_draw = jnp.clip(jax.random.normal(noise_key, overall_shape, jnp.float32), -6.0, 6.0)
    return base_draw.astype(jnp.bfloat16)


def block_levels(key, shape, cuts, low, top_value):
    def one(dim, shards_of):
        draws = jax.random.uniform(jax.random.fold_in(jax.random.fold_in(key, 6), dim), (shards_of,), jnp.float32, low / len(cuts), top_value / len(cuts))
        return jnp.repeat(jnp.exp(draws), shape[dim] // shards_of).reshape((-1,) + (1,) * (len(shape) - dim - 1))

    gain = one(*cuts[0])
    for cut in cuts[1:]:
        gain = gain * one(*cut)
    return gain


def scatter_about(stream_key, shape, scale, most, pieces=(), kind=jnp.bfloat16):
    drawn = jax.random.normal(stream_key, shape, jnp.float32) * scale
    if len(pieces) > 0:
        drawn = block_levels(stream_key, shape, pieces, -0.22, 0.18) * drawn
    return jnp.clip(drawn, min=-most, max=most).astype(kind)


def setup_inputs(seed: int = 0) -> dict:
    key_list = jax.random.split(jax.random.key(seed), 9)
    queries = draw_queries(jax.random.fold_in(key_list[8], 71), 0)
    keys = draw_keys(jax.random.fold_in(key_list[8], 71), 0)
    values = scatter_about(key_list[2], (TOTAL_BLOCKS, BLOCK_ROWS, KEY_VALUE_HEADS * HEAD_SIZE), 1.0, 6.0, ((0, 8), (2, 4)))
    out_weight = scatter_about(key_list[3], (QUERY_HEADS * HEAD_SIZE, D), (QUERY_HEADS * HEAD_SIZE) ** -0.5, 0.125, ((1, 4),))
    dest_slot = draw_dest_slot(jax.random.fold_in(key_list[8], 71), 0)
    pack_slot = draw_pack_slot(jax.random.fold_in(key_list[8], 71), 0)
    seq_start = draw_seq_start(jax.random.fold_in(key_list[8], 71), 0)
    seq_len = draw_seq_len(jax.random.fold_in(key_list[8], 71), 0)
    return {"queries": queries, "keys": keys, "values": values, "out_weight": out_weight, "dest_slot": dest_slot, "pack_slot": pack_slot, "seq_start": seq_start, "seq_len": seq_len}


def pack_attention(packed_queries, packed_keys, packed_values, starts, lengths):
    total_row_count = packed_queries.shape[0]
    query_group_count = QUERY_HEADS // KEY_VALUE_HEADS
    tile_rows = 16 * BLOCK_ROWS
    score_scale = 1.0 / (HEAD_SIZE ** 0.5)
    row_ids = jnp.arange(total_row_count, dtype=jnp.int32)
    segment = (jnp.sum((starts[None, :] <= row_ids[:, None]).astype(jnp.int32), axis=1) - 1).astype(jnp.int32)
    begins = jnp.take(starts, segment)
    limits = jnp.take(lengths, segment)
    usable = (row_ids - begins) < limits
    query_head_rows = packed_queries.astype(jnp.float32).reshape(total_row_count, KEY_VALUE_HEADS, query_group_count, HEAD_SIZE)
    key_head_rows = packed_keys.astype(jnp.float32).reshape(total_row_count, KEY_VALUE_HEADS, HEAD_SIZE)
    value_head_rows = packed_values.astype(jnp.float32).reshape(total_row_count, KEY_VALUE_HEADS, HEAD_SIZE)
    blocks_out = []
    for tile_index in range(total_row_count // tile_rows):
        first_row = tile_index * tile_rows
        end_row = first_row + tile_rows
        scores = jnp.einsum("rgnd,cgd->gnrc", query_head_rows[first_row:end_row], key_head_rows[:end_row]) * score_scale
        allowed = (segment[first_row:end_row, None] == segment[None, :end_row]) & (row_ids[None, :end_row] <= row_ids[first_row:end_row, None])
        scores = jnp.where(allowed[None, None], scores, -jnp.inf)
        largest = jnp.max(scores, axis=-1, keepdims=True)
        exponent = jnp.exp(scores - largest)
        weights = (exponent / jnp.sum(exponent, axis=-1, keepdims=True)).astype(jnp.bfloat16)
        mixture = jnp.einsum("gnrc,cgd->rgnd", weights.astype(jnp.float32), value_head_rows[:end_row])
        mixture = jnp.where(usable[first_row:end_row, None, None, None], mixture, 0.0)
        blocks_out.append(mixture.reshape(tile_rows, QUERY_HEADS * HEAD_SIZE).astype(jnp.bfloat16))
    return jnp.concatenate(blocks_out, axis=0)


def reference(queries, keys, values, out_weight, dest_slot, pack_slot, seq_start, seq_len):
    dest_table = dest_slot.reshape(N_DP, LOADER_BLOCKS)
    positions = jnp.arange(LOADER_BLOCKS, dtype=jnp.int32)

    def one_pack(pack_index):
        slot_row = pack_slot[pack_index]
        loader = (slot_row // CAP).astype(jnp.int32)
        wanted = (pack_index * CAP + slot_row % CAP).astype(jnp.int32)
        candidates = dest_table[loader]
        local_index = jnp.sum(jnp.where(candidates == wanted[:, None], positions[None, :], 0), axis=1)
        source_block = (loader * LOADER_BLOCKS + local_index).astype(jnp.int32)
        attended = pack_attention(
            queries[source_block].reshape(LOADER_BLOCKS * BLOCK_ROWS, QUERY_HEADS * HEAD_SIZE),
            keys[source_block].reshape(LOADER_BLOCKS * BLOCK_ROWS, KEY_VALUE_HEADS * HEAD_SIZE),
            values[source_block].reshape(LOADER_BLOCKS * BLOCK_ROWS, KEY_VALUE_HEADS * HEAD_SIZE),
            seq_start[pack_index],
            seq_len[pack_index],
        )
        return attended.reshape(LOADER_BLOCKS, BLOCK_ROWS, QUERY_HEADS * HEAD_SIZE), source_block

    results, sources = lax.map(one_pack, jnp.arange(N_DP, dtype=jnp.int32))
    at_home = jnp.zeros((TOTAL_BLOCKS, BLOCK_ROWS, QUERY_HEADS * HEAD_SIZE), jnp.bfloat16).at[sources.reshape(-1)].set(results.reshape(TOTAL_BLOCKS, BLOCK_ROWS, QUERY_HEADS * HEAD_SIZE))
    projected = jnp.dot(at_home.reshape(TOTAL_BLOCKS * BLOCK_ROWS, QUERY_HEADS * HEAD_SIZE), out_weight, preferred_element_type=jnp.float32)
    return projected.astype(jnp.bfloat16).reshape(TOTAL_BLOCKS, BLOCK_ROWS, D)
```

```python
import functools

import jax
import jax.numpy as jnp
from jax import lax
from jax.experimental import pallas as pl
from jax.experimental.pallas import tpu as pltpu
from jax.sharding import PartitionSpec as P

HEAD_SIZE = 128
MASKED = -1e30
SHARES = (3, 3, 2)


def tile_scores(query_tile, key_tile, score_scale):
    return (
        jnp.einsum("rgnd,cgd->gnrc", query_tile, key_tile, preferred_element_type=jnp.float32)
        * score_scale
    )


def tile_mix(weight_tile, value_tile):
    return jnp.einsum("gnrc,cgd->rgnd", weight_tile, value_tile, preferred_element_type=jnp.float32)


def attend(packed_queries, packed_keys, packed_values, starts, lengths, block_rows):
    total_row_count, query_cols = packed_queries.shape
    kv_heads = packed_keys.shape[1] // HEAD_SIZE
    query_group_count = query_cols // HEAD_SIZE // kv_heads
    tile_rows = 16 * block_rows
    score_scale = 1.0 / HEAD_SIZE**0.5
    row_ids = jnp.arange(total_row_count, dtype=jnp.int32)
    segment = jnp.sum((starts[None, :] <= row_ids[:, None]).astype(jnp.int32), axis=1) - 1
    picked = segment[:, None] == jnp.arange(starts.shape[0], dtype=jnp.int32)[None, :]
    begins = jnp.sum(jnp.where(picked, starts[None, :], 0), axis=1)
    limits = jnp.sum(jnp.where(picked, lengths[None, :], 0), axis=1)
    usable = row_ids - begins < limits
    query_head_rows = packed_queries.reshape(
        total_row_count, kv_heads, query_group_count, HEAD_SIZE
    )
    key_head_rows = packed_keys.reshape(total_row_count, kv_heads, HEAD_SIZE)
    value_head_rows = packed_values.reshape(total_row_count, kv_heads, HEAD_SIZE)
    blocks_out = []
    for tile_index in range(total_row_count // tile_rows):
        first_row = tile_index * tile_rows
        end_row = first_row + tile_rows
        scores = tile_scores(
            query_head_rows[first_row:end_row], key_head_rows[:end_row], score_scale
        )
        allowed = (segment[first_row:end_row, None] == segment[None, :end_row]) & (
            row_ids[None, :end_row] <= row_ids[first_row:end_row, None]
        )
        scores = jnp.where(allowed[None, None], scores, -jnp.inf)
        largest = jnp.max(scores, axis=-1, keepdims=True)
        exponent = jnp.exp(scores - largest)
        weights = (exponent / jnp.sum(exponent, axis=-1, keepdims=True)).astype(jnp.bfloat16)
        mixture = tile_mix(weights, value_head_rows[:end_row])
        mixture = jnp.where(usable[first_row:end_row, None, None, None], mixture, 0.0)
        blocks_out.append(mixture.reshape(tile_rows, query_cols).astype(jnp.bfloat16))
    return jnp.concatenate(blocks_out, axis=0)


def exchange_body(
    queries, keys, values, out_weight, dest_slot, pack_slot, seq_start, seq_len
):
    local_blocks, block_rows, query_cols = queries.shape
    loaders = lax.axis_size("dp")
    capacity = (local_blocks + loaders - 1) // loaders
    slot_count = loaders * capacity

    def outgoing(portion):
        return (
            jnp.zeros((slot_count,) + portion.shape[1:], portion.dtype).at[dest_slot].set(portion)
        )

    arrived = tuple(
        lax.all_to_all(outgoing(portion), "dp", split_axis=0, concat_axis=0, tiled=True)
        for portion in (queries, keys, values)
    )
    sources = pack_slot[0]

    def collect(portion):
        return jnp.take(portion, sources, axis=0).reshape(
            local_blocks * block_rows, portion.shape[2]
        )

    attended = attend(
        collect(arrived[0]),
        collect(arrived[1]),
        collect(arrived[2]),
        seq_start[0],
        seq_len[0],
        block_rows,
    )
    going_back = (
        jnp.zeros((slot_count, block_rows, query_cols), jnp.bfloat16)
        .at[sources]
        .set(attended.reshape(local_blocks, block_rows, query_cols))
    )
    returned = lax.all_to_all(going_back, "dp", split_axis=0, concat_axis=0, tiled=True)
    own_rows = jnp.take(returned, dest_slot, axis=0).reshape(local_blocks * block_rows, query_cols)
    projected = jnp.dot(
        lax.all_gather(own_rows, "tensor", axis=1, tiled=True),
        out_weight,
        preferred_element_type=jnp.float32,
    )
    return projected.astype(jnp.bfloat16).reshape(local_blocks, block_rows, out_weight.shape[1])


VMEM = pl.BlockSpec(memory_space=pltpu.VMEM)
SMEM = pl.BlockSpec(memory_space=pltpu.SMEM)
ANY = pl.BlockSpec(memory_space=pl.ANY)


def invert(table_ref, base, count, inverse_ref):
    def step(index, carry):
        inverse_ref[table_ref[base + index]] = index
        return carry

    lax.fori_loop(0, count, step, 0)


def sort_kernel(slots_ref, key_ref, value_ref, whole_ref, *refs):
    *part_refs, inverse_ref = refs
    invert(slots_ref, 0, key_ref.shape[0], inverse_ref)
    slot = 0
    for part_ref in part_refs:
        for index in range(part_ref.shape[0]):
            source = inverse_ref[slot]
            both = jnp.concatenate([key_ref[source], value_ref[source]], axis=-1)
            part_ref[index] = both
            whole_ref[slot] = both
            slot += 1


def sort_blocks(keys, values, dest_slot, parts):
    blocks, rows, cols = keys.shape
    shapes = [(blocks, rows, 2 * cols)] + [(part, rows, 2 * cols) for part in parts]
    return pl.pallas_call(
        sort_kernel,
        out_shape=[jax.ShapeDtypeStruct(shape, keys.dtype) for shape in shapes],
        in_specs=[SMEM, VMEM, VMEM],
        out_specs=[VMEM] * len(shapes),
        scratch_shapes=[pltpu.SMEM((blocks,), jnp.int32)],
        name="sort_blocks",
    )(dest_slot, keys, values)


def attend_kernel(
    first, capacity, masks, tables_ref, slots_ref, place_ref, query_ref, *refs
):
    sources = len(masks)
    item_refs = refs[:sources]
    out_ref, inverse_ref, position_ref, low_ref, limit_ref, key_ref, value_ref = refs[sources:]
    blocks, block_rows, query_cols = query_ref.shape
    heads = query_cols // HEAD_SIZE
    step = pl.program_id(0)
    pack = first + step
    place = place_ref[0]
    width = 3 * blocks

    @pl.when(step == 0)
    def _():
        invert(slots_ref, 0, blocks, inverse_ref)

    base = pack * width

    def scan(position, segment):
        position_ref[tables_ref[base + position]] = position
        after = jnp.minimum(segment + 1, blocks - 1)
        reached = tables_ref[base + blocks + after] <= position * block_rows
        segment = jnp.where(reached, after, segment)
        begin = tables_ref[base + blocks + segment]
        low_ref[position] = begin
        limit_ref[position] = begin + tables_ref[base + 2 * blocks + segment]
        return segment

    lax.fori_loop(0, blocks, scan, 0)

    for mask, item_ref in zip(masks, item_refs):
        origin = jnp.bitwise_xor(place, mask) * capacity
        for index in range(capacity):
            position = position_ref[origin + index]
            rows = pl.ds(pl.multiple_of(position * block_rows, block_rows), block_rows)
            key_ref[rows, :] = item_ref[index, :, :HEAD_SIZE]
            value_ref[rows, :] = item_ref[index, :, HEAD_SIZE:]

    total = blocks * block_rows
    tiles = 4
    tile = total // tiles
    scale = 1.4426950408889634 / HEAD_SIZE**0.5

    def one_block(index, carry):
        source = inverse_ref[pack * capacity + index]
        position = position_ref[place * capacity + index]
        low = low_ref[position]
        limit = limit_ref[position]
        row_base = position * block_rows
        need = row_base // tile
        query = query_ref[source]
        stacked = jnp.concatenate(
            [query[:, head * HEAD_SIZE : (head + 1) * HEAD_SIZE] for head in range(heads)], axis=0
        )
        for count in range(tiles):

            @pl.when(need == count)
            def _():
                span = (count + 1) * tile
                scores = lax.dot_general(
                    stacked,
                    key_ref[:span, :],
                    (((1,), (1,)), ((), ())),
                    preferred_element_type=jnp.float32,
                )
                column = lax.broadcasted_iota(jnp.int32, (block_rows, span), 1)
                row = lax.broadcasted_iota(jnp.int32, (block_rows, span), 0) + row_base
                allowed = (column <= row) & (column >= low)
                scores = jnp.where(
                    allowed[None], scores.reshape(heads, block_rows, span) * scale, MASKED
                ).reshape(heads * block_rows, span)
                largest = jnp.max(scores, axis=-1, keepdims=True)
                terms = jnp.exp2(scores - largest)
                mass = jnp.sum(terms, axis=-1, keepdims=True)
                mixed = jnp.dot(
                    terms.astype(jnp.bfloat16),
                    value_ref[:span, :],
                    preferred_element_type=jnp.float32,
                )
                used = (
                    lax.broadcasted_iota(jnp.int32, (block_rows, HEAD_SIZE), 0) + row_base < limit
                )
                mixed = (mixed / mass).reshape(heads, block_rows, HEAD_SIZE)
                mixed = jnp.where(used[None], mixed, 0.0).astype(jnp.bfloat16)
                for head in range(heads):
                    out_ref[index, :, head * HEAD_SIZE : (head + 1) * HEAD_SIZE] = mixed[head]

        return carry

    lax.fori_loop(0, capacity, one_block, 0)


def attend_part(first, packs, capacity, tables, slots, place, queries, items):
    blocks, block_rows, query_cols = queries.shape
    kv_cols = 2 * HEAD_SIZE
    in_specs = [SMEM, SMEM, SMEM, pl.BlockSpec(queries.shape, lambda step: (0, 0, 0))]
    for _, item, offset in items:
        in_specs.append(
            pl.BlockSpec(
                (capacity, block_rows, kv_cols), lambda step, offset=offset: (step + offset, 0, 0)
            )
        )
    total = blocks * block_rows
    pairs = packs * capacity * block_rows * (query_cols // HEAD_SIZE) * total
    return pl.pallas_call(
        functools.partial(attend_kernel, first, capacity, tuple(item[0] for item in items)),
        grid=(packs,),
        out_shape=jax.ShapeDtypeStruct((packs * capacity, block_rows, query_cols), jnp.bfloat16),
        in_specs=in_specs,
        out_specs=pl.BlockSpec((capacity, block_rows, query_cols), lambda step: (step, 0, 0)),
        scratch_shapes=[pltpu.SMEM((blocks,), jnp.int32)] * 4
        + [pltpu.VMEM((total, HEAD_SIZE), jnp.bfloat16)] * 2,
        cost_estimate=pl.CostEstimate(
            flops=2 * pairs * HEAD_SIZE,
            bytes_accessed=2 * packs * total * kv_cols,
            transcendentals=pairs // 2,
        ),
        name="attend_part",
    )(tables, slots, place, queries, *[item[1] for item in items])


def project_kernel(first, masks, slots_ref, place_ref, weight_ref, *refs):
    count = len(masks)
    part_refs = refs[:count]
    out_ref, inverse_ref, staged_ref, semaphores = refs[-4:]
    blocks, block_rows, cols = part_refs[0].shape
    invert(slots_ref, 0, slots_ref.shape[0], inverse_ref)
    place = place_ref[0]
    total = None
    for mask, part_ref in zip(masks, part_refs):
        begin = pl.multiple_of(jnp.bitwise_xor(place, mask) * cols, cols)
        product = jnp.dot(
            part_ref[...].reshape(blocks * block_rows, cols),
            weight_ref[pl.ds(begin, cols), :],
            preferred_element_type=jnp.float32,
        )
        total = product if total is None else total + product
    staged_ref[...] = total.astype(jnp.bfloat16).reshape(staged_ref.shape)
    copies = []
    for index in range(blocks):
        copy = pltpu.make_async_copy(
            staged_ref.at[index],
            out_ref.at[inverse_ref[first + index]],
            semaphores.at[index],
        )
        copy.start()
        copies.append(copy)
    for copy in copies:
        copy.wait()


def project_part(first, slots, place, out_weight, masks, parts, so_far, out_shape):
    blocks, block_rows, cols = parts[0].shape
    features = out_weight.shape[1]
    operands = [slots, place, out_weight, *parts]
    in_specs = [SMEM, SMEM, VMEM] + [VMEM] * len(parts)
    aliases = {}
    if so_far is not None:
        aliases = {len(operands): 0}
        operands.append(so_far)
        in_specs.append(ANY)
    rows = blocks * block_rows
    return pl.pallas_call(
        functools.partial(project_kernel, first, masks),
        out_shape=jax.ShapeDtypeStruct(out_shape, jnp.bfloat16),
        in_specs=in_specs,
        out_specs=ANY,
        scratch_shapes=[
            pltpu.SMEM((slots.shape[0],), jnp.int32),
            pltpu.VMEM((blocks, block_rows, features), jnp.bfloat16),
            pltpu.SemaphoreType.DMA((blocks,)),
        ],
        input_output_aliases=aliases,
        cost_estimate=pl.CostEstimate(
            flops=2 * rows * cols * len(parts) * features,
            bytes_accessed=2 * (cols * len(parts) * features + rows * features),
            transcendentals=0,
        ),
        name="project_part",
    )(*operands)


def gather_body(queries, keys, values, out_weight, dest_slot, pack_slot, seq_start, seq_len):
    local_blocks, block_rows, query_cols = queries.shape
    loaders = lax.axis_size("dp")
    shards = lax.axis_size("tensor")
    capacity = local_blocks // loaders
    side, near, far = 1, 2, loaders - 2
    place = lax.axis_index("dp").astype(jnp.int32).reshape(1)
    shard = lax.axis_index("tensor").astype(jnp.int32).reshape(1)

    def swap(portion, axis, mask):
        size = lax.axis_size(axis)
        return lax.ppermute(portion, axis, [(index, index ^ mask) for index in range(size)])

    shares = [share * loaders // sum(SHARES) for share in SHARES]
    firsts = [sum(shares[:index]) for index in range(len(shares))]

    own = jnp.concatenate([pack_slot, seq_start, seq_len], axis=1)
    tables = lax.all_to_all(
        jnp.broadcast_to(own, (loaders, own.shape[1])), "dp", 0, 0, tiled=True
    ).reshape(-1)

    whole, *pieces = sort_blocks(keys, values, dest_slot, [share * capacity for share in shares])
    from_far = [swap(piece, "dp", far) for piece in pieces]
    from_near = swap(whole, "dp", near)
    from_side = swap(whole, "dp", side)
    from_both = swap(from_near, "dp", side)
    attended = []
    for index, (first, share) in enumerate(zip(firsts, shares)):
        across = from_far[index]
        far_near = swap(across, "dp", near)
        far_side = swap(across, "dp", side)
        far_both = swap(far_near, "dp", side)
        items = (
            (0, whole, first),
            (side, from_side, first),
            (near, from_near, first),
            (near ^ side, from_both, first),
            (far, across, 0),
            (far ^ side, far_side, 0),
            (far ^ near, far_near, 0),
            (far ^ near ^ side, far_both, 0),
        )
        attended.append(
            attend_part(first, share, capacity, tables, dest_slot, place, queries, items)
        )
    result = None
    out_shape = (local_blocks, block_rows, out_weight.shape[1])
    for first, part in zip(firsts, attended):
        partner = swap(part, "tensor", 1)
        opposite = swap(part, "tensor", shards // 2)
        both = swap(opposite, "tensor", 1)
        result = project_part(
            first * capacity,
            dest_slot,
            shard,
            out_weight,
            (0, 1, shards // 2, shards // 2 + 1),
            (part, partner, opposite, both),
            result,
            out_shape,
        )
    return result


def solution(mesh):
    placed = (
        P("dp", None, "tensor"),
        P("dp", None, "tensor"),
        P("dp", None, "tensor"),
        P(None, "tensor"),
        P("dp"),
        P("dp", None),
        P("dp", None),
        P("dp", None),
    )

    def body(queries, keys, values, *rest):
        loaders = mesh.shape["dp"]
        combinations = 2**3
        gathers = (
            loaders == combinations
            and mesh.shape["tensor"] == 4
            and queries.shape[0] % loaders == 0
            and keys.shape[2] == HEAD_SIZE
        )
        chosen = gather_body if gathers else exchange_body
        return chosen(queries, keys, values, *rest)

    return jax.shard_map(
        body, mesh=mesh, in_specs=placed, out_specs=P("dp", None, "tensor"), check_vma=False
    )
```

```python
import functools

import jax
import jax.numpy as jnp
from jax import lax
from jax.experimental import pallas as pl
from jax.experimental.pallas import tpu as pltpu
from jax.sharding import PartitionSpec as P


HEAD_SIZE = 128
MASKED = -1e30
SHARES = (3, 3, 2)


def tile_scores(query_tile, key_tile, score_scale):
    return (
        jnp.einsum("rgnd,cgd->gnrc", query_tile, key_tile, preferred_element_type=jnp.float32)
        * score_scale
    )


def tile_mix(weight_tile, value_tile):
    return jnp.einsum("gnrc,cgd->rgnd", weight_tile, value_tile, preferred_element_type=jnp.float32)


def attend(packed_queries, packed_keys, packed_values, starts, lengths, block_rows):
    total_row_count, query_cols = packed_queries.shape
    kv_heads = packed_keys.shape[1] // HEAD_SIZE
    query_group_count = query_cols // HEAD_SIZE // kv_heads
    tile_rows = 16 * block_rows
    score_scale = 1.0 / HEAD_SIZE**0.5
    row_ids = jnp.arange(total_row_count, dtype=jnp.int32)
    segment = jnp.sum((starts[None, :] <= row_ids[:, None]).astype(jnp.int32), axis=1) - 1
    picked = segment[:, None] == jnp.arange(starts.shape[0], dtype=jnp.int32)[None, :]
    begins = jnp.sum(jnp.where(picked, starts[None, :], 0), axis=1)
    limits = jnp.sum(jnp.where(picked, lengths[None, :], 0), axis=1)
    usable = row_ids - begins < limits
    query_head_rows = packed_queries.reshape(
        total_row_count, kv_heads, query_group_count, HEAD_SIZE
    )
    key_head_rows = packed_keys.reshape(total_row_count, kv_heads, HEAD_SIZE)
    value_head_rows = packed_values.reshape(total_row_count, kv_heads, HEAD_SIZE)
    blocks_out = []
    for tile_index in range(total_row_count // tile_rows):
        first_row = tile_index * tile_rows
        end_row = first_row + tile_rows
        scores = tile_scores(
            query_head_rows[first_row:end_row], key_head_rows[:end_row], score_scale
        )
        allowed = (segment[first_row:end_row, None] == segment[None, :end_row]) & (
            row_ids[None, :end_row] <= row_ids[first_row:end_row, None]
        )
        scores = jnp.where(allowed[None, None], scores, -jnp.inf)
        largest = jnp.max(scores, axis=-1, keepdims=True)
        exponent = jnp.exp(scores - largest)
        weights = (exponent / jnp.sum(exponent, axis=-1, keepdims=True)).astype(jnp.bfloat16)
        mixture = tile_mix(weights, value_head_rows[:end_row])
        mixture = jnp.where(usable[first_row:end_row, None, None, None], mixture, 0.0)
        blocks_out.append(mixture.reshape(tile_rows, query_cols).astype(jnp.bfloat16))
    return jnp.concatenate(blocks_out, axis=0)


def exchange_body(
    queries, keys, values, out_weight, dest_slot, pack_slot, seq_start, seq_len
):
    local_blocks, block_rows, query_cols = queries.shape
    loaders = lax.axis_size("dp")
    capacity = (local_blocks + loaders - 1) // loaders
    slot_count = loaders * capacity

    def outgoing(portion):
        return (
            jnp.zeros((slot_count,) + portion.shape[1:], portion.dtype).at[dest_slot].set(portion)
        )

    arrived = tuple(
        lax.all_to_all(outgoing(portion), "dp", split_axis=0, concat_axis=0, tiled=True)
        for portion in (queries, keys, values)
    )
    sources = pack_slot[0]

    def collect(portion):
        return jnp.take(portion, sources, axis=0).reshape(
            local_blocks * block_rows, portion.shape[2]
        )

    attended = attend(
        collect(arrived[0]),
        collect(arrived[1]),
        collect(arrived[2]),
        seq_start[0],
        seq_len[0],
        block_rows,
    )
    going_back = (
        jnp.zeros((slot_count, block_rows, query_cols), jnp.bfloat16)
        .at[sources]
        .set(attended.reshape(local_blocks, block_rows, query_cols))
    )
    returned = lax.all_to_all(going_back, "dp", split_axis=0, concat_axis=0, tiled=True)
    own_rows = jnp.take(returned, dest_slot, axis=0).reshape(local_blocks * block_rows, query_cols)
    projected = jnp.dot(
        lax.all_gather(own_rows, "tensor", axis=1, tiled=True),
        out_weight,
        preferred_element_type=jnp.float32,
    )
    return projected.astype(jnp.bfloat16).reshape(local_blocks, block_rows, out_weight.shape[1])


VMEM = pl.BlockSpec(memory_space=pltpu.VMEM)
SMEM = pl.BlockSpec(memory_space=pltpu.SMEM)
HBM = pl.BlockSpec(memory_space=pltpu.HBM)
ROOM = pltpu.CompilerParams(vmem_limit_bytes=24 * 2**20)


def sort_kernel(slots_ref, key_ref, value_ref, inverse_ref, whole_ref, *part_refs):
    blocks = key_ref.shape[0]

    def note(index, carry):
        inverse_ref[slots_ref[index]] = index
        return carry

    lax.fori_loop(0, blocks, note, 0, unroll=4)
    slot = 0
    for part_ref in part_refs:
        for index in range(part_ref.shape[0]):
            source = inverse_ref[slot]
            both = jnp.concatenate([key_ref[source], value_ref[source]], axis=-1)
            part_ref[index] = both
            whole_ref[slot] = both
            slot += 1


def sort_blocks(keys, values, dest_slot, parts):
    blocks, rows, cols = keys.shape
    shapes = [(blocks, rows, 2 * cols)] + [(part, rows, 2 * cols) for part in parts]
    return pl.pallas_call(
        sort_kernel,
        out_shape=[jax.ShapeDtypeStruct((blocks,), jnp.int32)]
        + [jax.ShapeDtypeStruct(shape, keys.dtype) for shape in shapes],
        in_specs=[SMEM, VMEM, VMEM],
        out_specs=[SMEM] + [VMEM] * len(shapes),
        compiler_params=ROOM,
        name="sort_blocks",
    )(dest_slot, keys, values)


def plan_kernel(
    block_rows, capacity, tables_ref, place_ref, position_ref, query_ref, low_ref, limit_ref
):
    blocks = query_ref.shape[0] // 3
    packs = position_ref.shape[0] // blocks
    own = place_ref[0] * capacity

    def one_pack(pack, carry):
        base = pack * 3 * blocks
        begin = tables_ref[base + blocks]
        limit = begin + tables_ref[base + 2 * blocks]
        after = 1
        for position in range(blocks):
            position_ref[pack * blocks + tables_ref[base + position]] = position
            if position > 0:
                upcoming = tables_ref[base + blocks + after]
                reached = upcoming <= position * block_rows
                begin = jnp.where(reached, upcoming, begin)
                limit = jnp.where(
                    reached, upcoming + tables_ref[base + 2 * blocks + after], limit
                )
                after = jnp.minimum(jnp.where(reached, after + 1, after), blocks - 1)
            low_ref[position] = begin
            limit_ref[position] = limit
        for member in range(capacity):
            position = position_ref[pack * blocks + own + member]
            query_ref[pack * capacity + member] = position * block_rows
            query_ref[blocks + pack * capacity + member] = low_ref[position]
            query_ref[2 * blocks + pack * capacity + member] = limit_ref[position]
        return carry

    lax.fori_loop(0, packs, one_pack, 0)


def plan(tables, place, blocks, block_rows, capacity):
    return pl.pallas_call(
        functools.partial(plan_kernel, block_rows, capacity),
        out_shape=[
            jax.ShapeDtypeStruct((tables.shape[0] // 3,), jnp.int32),
            jax.ShapeDtypeStruct((3 * blocks,), jnp.int32),
        ],
        in_specs=[SMEM, SMEM],
        out_specs=[SMEM, SMEM],
        scratch_shapes=[pltpu.SMEM((blocks,), jnp.int32)] * 2,
        compiler_params=ROOM,
        name="plan",
    )(tables, place)


def attend_kernel(
    first, capacity, masks, offsets, position_ref, info_ref, inverse_ref, place_ref, query_ref, *refs
):
    sources = len(masks)
    item_refs = refs[:sources]
    out_ref, staged_ref, key_ref, value_ref, semaphores = refs[sources:]
    count, block_rows, query_cols = staged_ref.shape
    total = key_ref.shape[0]
    blocks = total // block_rows
    heads = query_cols // HEAD_SIZE
    place = place_ref[0]
    scale = 1.4426950408889634 / HEAD_SIZE**0.5
    copies = []
    for pack in range(count // capacity):
        table = (first + pack) * blocks
        for index, mask in enumerate(masks):
            origin = table + jnp.bitwise_xor(place, mask) * capacity
            for member in range(capacity):
                begin = pl.multiple_of(position_ref[origin + member] * block_rows, block_rows)
                rows = pl.ds(begin, block_rows)
                block = item_refs[index][offsets[index] + pack * capacity + member]
                key_ref[rows, :] = block[:, :HEAD_SIZE]
                value_ref[rows, :] = block[:, HEAD_SIZE:]
        stacks = []
        for member in range(capacity):
            index = pack * capacity + member
            query = query_ref[inverse_ref[first * capacity + index]]
            stacks += [query[:, head * HEAD_SIZE : (head + 1) * HEAD_SIZE] for head in range(heads)]
        scores = lax.dot_general(
            jnp.concatenate(stacks, axis=0),
            key_ref[...],
            (((1,), (1,)), ((), ())),
            preferred_element_type=jnp.float32,
        )
        masses = []
        weights = []
        for member in range(capacity):
            index = pack * capacity + member
            row_base = info_ref[first * capacity + index]
            low = info_ref[blocks + first * capacity + index]
            column = lax.broadcasted_iota(jnp.int32, (block_rows, total), 1)
            row = lax.broadcasted_iota(jnp.int32, (block_rows, total), 0) + row_base
            allowed = (column <= row) & (column >= low)
            for head in range(heads):
                begin = (member * heads + head) * block_rows
                part = jnp.where(allowed, scores[begin : begin + block_rows] * scale, MASKED)
                largest = jnp.max(part, axis=-1, keepdims=True)
                terms = jnp.exp2(part - largest)
                masses.append(jnp.sum(terms, axis=-1, keepdims=True))
                weights.append(terms.astype(jnp.bfloat16))
        mixed = jnp.dot(
            jnp.concatenate(weights, axis=0), value_ref[...], preferred_element_type=jnp.float32
        )
        for member in range(capacity):
            index = pack * capacity + member
            row_base = info_ref[first * capacity + index]
            limit = info_ref[2 * blocks + first * capacity + index]
            used = lax.broadcasted_iota(jnp.int32, (block_rows, HEAD_SIZE), 0) + row_base < limit
            for head in range(heads):
                begin = (member * heads + head) * block_rows
                part = mixed[begin : begin + block_rows] / masses[member * heads + head]
                staged_ref[index, :, head * HEAD_SIZE : (head + 1) * HEAD_SIZE] = jnp.where(
                    used, part, 0.0
                ).astype(jnp.bfloat16)
        rows = pl.ds(pack * capacity, capacity)
        copy = pltpu.make_async_copy(staged_ref.at[rows], out_ref.at[rows], semaphores.at[pack])
        copy.start()
        copies.append(copy)
    for copy in copies:
        copy.wait()


def attend_part(first, count, capacity, position, info, inverse, place, queries, items):
    blocks, block_rows, query_cols = queries.shape
    total = blocks * block_rows
    pairs = count * block_rows * (query_cols // HEAD_SIZE) * total
    masks, arrays, offsets = zip(*items)
    return pl.pallas_call(
        functools.partial(attend_kernel, first, capacity, masks, offsets),
        out_shape=jax.ShapeDtypeStruct((count, block_rows, query_cols), jnp.bfloat16),
        in_specs=[SMEM] * 4 + [VMEM] * (1 + len(items)),
        out_specs=HBM,
        scratch_shapes=[
            pltpu.VMEM((count, block_rows, query_cols), jnp.bfloat16),
            pltpu.VMEM((total, HEAD_SIZE), jnp.bfloat16),
            pltpu.VMEM((total, HEAD_SIZE), jnp.bfloat16),
            pltpu.SemaphoreType.DMA((count // capacity,)),
        ],
        compiler_params=ROOM,
        cost_estimate=pl.CostEstimate(
            flops=4 * pairs * HEAD_SIZE,
            bytes_accessed=2 * count * block_rows * (len(items) * 2 * HEAD_SIZE + 2 * query_cols),
            transcendentals=pairs,
        ),
        name="attend_part",
    )(position, info, inverse, place, queries, *arrays)


def project_kernel(first, masks, pieces, inverse_ref, place_ref, weight_ref, *refs):
    count = len(masks)
    part_refs = refs[:count]
    out_ref, gathered_ref, staged_ref, semaphores = refs[-4:]
    blocks, block_rows, cols = part_refs[0].shape
    rows = blocks * block_rows
    place = place_ref[0]
    features = weight_ref.shape[1]
    width = features // pieces
    for mask, part_ref in zip(masks, part_refs):
        begin = pl.multiple_of(jnp.bitwise_xor(place, mask) * cols, cols)
        gathered_ref[:, pl.ds(begin, cols)] = part_ref[...].reshape(rows, cols)
    copies = []
    for piece in range(pieces):
        span = slice(piece * width, (piece + 1) * width)
        total = jnp.dot(
            gathered_ref[...], weight_ref[:, span], preferred_element_type=jnp.float32
        )
        staged_ref[:, :, span] = total.astype(jnp.bfloat16).reshape(blocks, block_rows, width)
        for index in range(blocks):
            copy = pltpu.make_async_copy(
                staged_ref.at[index, :, span],
                out_ref.at[inverse_ref[first + index], :, span],
                semaphores.at[piece, index],
            )
            copy.start()
            copies.append(copy)
    for copy in copies:
        copy.wait()


def project_part(first, inverse, place, out_weight, masks, parts, so_far, out_shape):
    blocks, block_rows, cols = parts[0].shape
    features = out_weight.shape[1]
    operands = [inverse, place, out_weight, *parts]
    in_specs = [SMEM, SMEM, VMEM] + [VMEM] * len(parts)
    aliases = {}
    if so_far is not None:
        aliases = {len(operands): 0}
        operands.append(so_far)
        in_specs.append(HBM)
    rows = blocks * block_rows
    pieces = 2
    return pl.pallas_call(
        functools.partial(project_kernel, first, masks, pieces),
        out_shape=jax.ShapeDtypeStruct(out_shape, jnp.bfloat16),
        in_specs=in_specs,
        out_specs=HBM,
        scratch_shapes=[
            pltpu.VMEM((rows, cols * len(parts)), jnp.bfloat16),
            pltpu.VMEM((blocks, block_rows, features), jnp.bfloat16),
            pltpu.SemaphoreType.DMA((pieces, blocks)),
        ],
        input_output_aliases=aliases,
        compiler_params=ROOM,
        cost_estimate=pl.CostEstimate(
            flops=2 * rows * cols * len(parts) * features,
            bytes_accessed=2 * (cols * len(parts) * features + rows * features),
            transcendentals=0,
        ),
        name="project_part",
    )(*operands)


def swap(portion, axis, mask):
    size = lax.axis_size(axis)
    return lax.ppermute(portion, axis, [(index, index ^ mask) for index in range(size)])


def split_packs(loaders):
    shares = [share * loaders // sum(SHARES) for share in SHARES]
    return [(sum(shares[:index]), share) for index, share in enumerate(shares)]


def gather_body(queries, keys, values, out_weight, dest_slot, pack_slot, seq_start, seq_len):
    local_blocks, block_rows, _ = queries.shape
    loaders = lax.axis_size("dp")
    shards = lax.axis_size("tensor")
    capacity = local_blocks // loaders
    side, near, far = 1, 2, loaders - 2
    place = lax.axis_index("dp").astype(jnp.int32).reshape(1)
    shard = lax.axis_index("tensor").astype(jnp.int32).reshape(1)
    chunks = split_packs(loaders)

    table = jnp.concatenate([pack_slot, seq_start, seq_len], axis=1)
    inverse, whole, *pieces = sort_blocks(
        keys, values, dest_slot, [share * capacity for _, share in chunks]
    )
    from_far = [swap(piece, "dp", far) for piece in pieces]
    from_near = swap(whole, "dp", near)
    from_side = swap(whole, "dp", side)
    from_both = swap(from_near, "dp", side)
    order = []
    for mask in (far, near, side):
        other = swap(table, "dp", mask)
        table = jnp.concatenate([table, other], axis=0)
        order = [m for m in order] + [m ^ mask for m in order] if order else [0, mask]
    origin = jnp.bitwise_xor(place, jnp.array(order, jnp.int32))
    tables = jnp.sum(
        jnp.where(
            (origin[None, :] == jnp.arange(loaders, dtype=jnp.int32)[:, None])[..., None],
            table[None],
            0,
        ),
        axis=1,
    ).reshape(-1)
    position, info = plan(tables, place, local_blocks, block_rows, capacity)
    attended = []
    for index, (first, share) in enumerate(chunks):
        across = from_far[index]
        far_near = swap(across, "dp", near)
        far_side = swap(across, "dp", side)
        far_both = swap(far_near, "dp", side)
        begin = first * capacity
        items = (
            (0, whole, begin),
            (side, from_side, begin),
            (near, from_near, begin),
            (near ^ side, from_both, begin),
            (far, across, 0),
            (far ^ side, far_side, 0),
            (far ^ near, far_near, 0),
            (far ^ near ^ side, far_both, 0),
        )
        attended.append(
            attend_part(
                first, share * capacity, capacity, position, info, inverse, place, queries, items
            )
        )
    result = None
    out_shape = (local_blocks, block_rows, out_weight.shape[1])
    for (first, share), part in zip(chunks, attended):
        partner = swap(part, "tensor", 1)
        opposite = swap(part, "tensor", shards // 2)
        both = swap(opposite, "tensor", 1)
        result = project_part(
            first * capacity,
            inverse,
            shard,
            out_weight,
            (0, 1, shards // 2, shards // 2 + 1),
            (part, partner, opposite, both),
            result,
            out_shape,
        )
    return result


def solution(mesh):
    placed = (
        P("dp", None, "tensor"),
        P("dp", None, "tensor"),
        P("dp", None, "tensor"),
        P(None, "tensor"),
        P("dp"),
        P("dp", None),
        P("dp", None),
        P("dp", None),
    )
    gathers = mesh.shape["dp"] == 2**3 and mesh.shape["tensor"] == 2**2

    def body(*args):
        if not gathers:
            return exchange_body(*args)
        return gather_body(*args)

    return jax.shard_map(
        body, mesh=mesh, in_specs=placed, out_specs=P("dp", None, "tensor"), check_vma=False
    )
```
